768 devices in a mesh: seq: 192 (over z, y_lo, x, core), dp: 4 (over y_hi).
Axes of the slice: x: 4, y: 8 (y_hi: 4, y_lo: 2; y = y_hi * 2 + y_lo), z: 12, core: 2. Of those that a mesh axis runs over, the one named last changes fastest.
Arguments:
- queries: bfloat16 [4, 24576, 4096], P('dp', 'seq'), may hold values from -4.5 to 4.5
- context: bfloat16 [4, 24576, 1024], P('dp', 'seq'), may hold values from -4.5 to 4.5
- segment_start: int32 [4, 24576], P('dp', 'seq'), may hold values from 0 to 24575, as said below
- memory: bfloat16 [4, 192, 64, 1024], P('dp', 'seq'), may hold values from -4.5 to 4.5
- image_offset: int32 [4, 192], P('dp', 'seq'), may hold values from 0 to 128, as said below
- cross_gate: float32 [32], replicated, may hold values from -1.5 to 1.5
- out_grad: bfloat16 [4, 24576, 4096], P('dp', 'seq'), may hold values from -6 to 6
Outputs:
- query_grad: bfloat16 [4, 24576, 4096], P('dp', 'seq')
- context_grad: bfloat16 [4, 24576, 1024], P('dp', 'seq')
- memory_grad: bfloat16 [4, 192, 64, 1024], P('dp', 'seq')
- gate_grad: float32 [32], replicated
The draws below stay inside these ranges and needn't reach their ends.
Inputs may be any that keep to these rules, and one draw needn't show every extreme that they name: `segment_start`: position of the first token of each token's segment: non-decreasing, equal to the position itself at a segment's first token; positions 0 and 24575 begin segments. `image_offset`: in each aligned block of 4 shards exactly one shard owns an image (offset below 128); every token that reads an image reads one owned at most 7 shards before its own, and that distance is reached in every draw.
All inputs are finite; a program needn't handle non-finite values.
Results may differ from the reference program's by a relative error of at most 0.012.
The reference program's roundings to bfloat16 on the way (of `narrow_weights`, `self_out`, `cross_narrow`, `grad_cross`, `grad_scores` and `grad_self`) count: a program that leaves them out, or rounds other values in their place, can miss the bound.
Values may be sent and summed in bfloat16 or wider, within the bound.
A program may use at most 128 MiB of HBM per device.

```python
import math
import jax
import jax.numpy as jnp
from jax import lax

HEADS = 32
KV_HEADS = 4
HEAD_DIM = 128
TOK_DEV = 128
IMG_TOK = 64
GAP = 4
WINDOW = 64
SHARDS = 192
SEQ = 24576
DOCS = 4


def base_law(key, shape):
    values = jnp.clip(jax.random.normal(key, shape, jnp.float32), -4.5, 4.5)
    return values


def draw_queries(key, part):
    values = base_law(jax.random.fold_in(key, 1), (DOCS, SEQ, HEADS * HEAD_DIM))
    return values.astype(jnp.bfloat16)


def draw_context(key, part):
    values = base_law(jax.random.fold_in(key, 2), (DOCS, SEQ, 2 * KV_HEADS * HEAD_DIM))
    return values.astype(jnp.bfloat16)


def draw_memory(key, part):
    values = base_law(jax.random.fold_in(key, 3), (DOCS, SHARDS, IMG_TOK, 2 * KV_HEADS * HEAD_DIM))
    return values.astype(jnp.bfloat16)


def draw_image_offset(key, part):
    blocks = SHARDS // GAP
    middle = SHARDS // 2 // GAP
    block_ids = jnp.arange(blocks, dtype=jnp.int32)
    slot = jax.random.randint(jax.random.fold_in(key, 21), (DOCS, blocks), 0, GAP)
    last_slot = (block_ids == 1) | (block_ids == middle - 1)
    first_slot = (block_ids == 0) | (block_ids == middle)
    slot = jnp.where(first_slot[None, :], 0, jnp.where(last_slot[None, :], GAP - 1, slot))
    first = jax.random.randint(jax.random.fold_in(key, 22), (DOCS, blocks), 0, TOK_DEV)
    later_first = jax.random.randint(jax.random.fold_in(key, 23), (DOCS, blocks), 1, TOK_DEV)
    first = jnp.where(((block_ids == 1) | (block_ids == middle))[None, :], later_first, first)
    shard_ids = jnp.arange(SHARDS, dtype=jnp.int32)
    block_of = shard_ids // GAP
    within = shard_ids % GAP
    owns = slot[:, block_of] == within[None, :]
    return jnp.where(owns, first[:, block_of], TOK_DEV).astype(jnp.int32)


def draw_segment_start(key, part):
    positions = jnp.arange(SEQ, dtype=jnp.int32)
    starts_here = jax.random.randint(jax.random.fold_in(key, 31), (DOCS, SEQ), 0, 160) == 0
    starts_here = starts_here | (positions == 0)[None, :] | (positions == SEQ - 1)[None, :]
    return lax.cummax(jnp.where(starts_here, positions[None, :], 0), axis=1).astype(jnp.int32)


def steps_of(stream_key, extent, pieces, low, top_value):
    def one(dim, blocks):
        heights = jax.random.uniform(jax.random.fold_in(jax.random.fold_in(stream_key, 6), dim), (blocks,), jnp.float32, low / len(pieces), top_value / len(pieces))
        return jnp.repeat(jnp.exp(heights), extent[dim] // blocks).reshape((-1,) + (1,) * (len(extent) - dim - 1))

    loudness = one(*pieces[0])
    for cut in pieces[1:]:
        loudness = loudness * one(*cut)
    return loudness


def noise(own_key, extent, scale, most, shards=(), held_as=jnp.bfloat16):
    gain = steps_of(own_key, extent, shards, -0.22, 0.18) if shards else 1.0
    drawn = jax.random.normal(own_key, extent, jnp.float32) * scale * gain
    return jnp.minimum(jnp.maximum(drawn, -most), most).astype(held_as)


def setup_inputs(seed: int = 0) -> dict:
    splits = jax.random.split(jax.random.key(seed), 8)
    return {
        "queries": draw_queries(jax.random.fold_in(splits[7], 71), 0),
        "context": draw_context(jax.random.fold_in(splits[7], 71), 0),
        "segment_start": draw_segment_start(jax.random.fold_in(splits[7], 71), 0),
        "memory": draw_memory(jax.random.fold_in(splits[7], 71), 0),
        "image_offset": draw_image_offset(jax.random.fold_in(splits[7], 71), 0),
        "cross_gate": jnp.clip(jax.random.uniform(splits[5], (HEADS,), jnp.float32, -1.5, 1.5), -1.5, 1.5),
        "out_grad": noise(splits[6], (DOCS, SEQ, HEADS * HEAD_DIM), 1.0, 6.0, ((0, 4), (1, 192))),
    }


def rounded(values):
    return lax.optimization_barrier(values.astype(jnp.bfloat16)).astype(jnp.float32)

def masked_softmax(scores, allowed):
    scores = jnp.where(allowed, scores, -1e+30)
    row_top = lax.optimization_barrier(jnp.max(scores, axis=-1, keepdims=True))
    powers = jnp.exp(scores - row_top)
    return powers / lax.optimization_barrier(jnp.sum(powers, axis=-1, keepdims=True))

def attend(query_heads, key_part, value_part, allowed):
    score_scale = 1.0 / math.sqrt(HEAD_DIM)
    scores = jnp.einsum('tgrd,kgd->grtk', query_heads, key_part) * score_scale
    weights = masked_softmax(scores, allowed[None, None])
    narrow_weights = rounded(weights)
    mixed = jnp.einsum('grtk,kgd->tgrd', narrow_weights, value_part)
    return (weights, narrow_weights, mixed)

def attend_back(grad_mixed, query_heads, key_part, value_part, weights, narrow_weights):
    score_scale = 1.0 / math.sqrt(HEAD_DIM)
    grad_weights = jnp.einsum('tgrd,kgd->grtk', grad_mixed, value_part)
    row_delta = lax.optimization_barrier(jnp.sum(weights * grad_weights, axis=-1, keepdims=True))
    grad_scores = rounded(weights * (grad_weights - row_delta))
    grad_queries = jnp.einsum('grtk,kgd->tgrd', grad_scores, key_part) * score_scale
    grad_keys = jnp.einsum('grtk,tgrd->kgd', grad_scores, query_heads) * score_scale
    grad_values = jnp.einsum('grtk,tgrd->kgd', narrow_weights, grad_mixed)
    return (grad_queries, grad_keys, grad_values)

def split_pair(joined):
    key_width = KV_HEADS * HEAD_DIM
    key_part = joined[:, :key_width].reshape(-1, KV_HEADS, HEAD_DIM)
    value_part = joined[:, key_width:].reshape(-1, KV_HEADS, HEAD_DIM)
    return (key_part, value_part)

def self_mask(shard_index, tok_rows, segment_row):
    query_pos = shard_index * tok_rows + jnp.arange(tok_rows, dtype=jnp.int32)
    key_pos = shard_index * tok_rows - WINDOW + jnp.arange(WINDOW + tok_rows, dtype=jnp.int32)
    return (key_pos[None, :] <= query_pos[:, None]) & (key_pos[None, :] >= query_pos[:, None] - WINDOW) & (key_pos[None, :] >= segment_row[:, None])

def cross_mask(tok_rows, offset, is_owner, has_prev):
    local = jnp.arange(tok_rows, dtype=jnp.int32)
    use_own = is_owner & (local >= offset)
    use_prev = jnp.logical_not(use_own) & has_prev
    columns = jnp.arange(2 * IMG_TOK, dtype=jnp.int32)
    allowed = jnp.where(columns[None, :] < IMG_TOK, use_prev[:, None], use_own[:, None])
    return (allowed, (use_own | use_prev).astype(jnp.float32))

def shard_pass(query_rows, joined_keys, joined_memory, allowed, cross_allowed, has_image, cross_gate, grad_rows):
    tok_rows = query_rows.shape[0]
    key_rows = joined_keys.shape[0]
    repeat = HEADS // KV_HEADS
    query_heads = query_rows.astype(jnp.float32).reshape(tok_rows, KV_HEADS, repeat, HEAD_DIM)
    key_part, value_part = split_pair(joined_keys.astype(jnp.float32))
    weights, narrow_weights, mixed = attend(query_heads, key_part, value_part, allowed)
    self_out = rounded(mixed)
    memory_keys, memory_values = split_pair(joined_memory.astype(jnp.float32))
    cross_weights, cross_narrow, cross_mixed = attend(self_out, memory_keys, memory_values, cross_allowed)
    image_mask = has_image[:, None, None, None]
    cross_mixed = cross_mixed * image_mask
    gate_tanh = jnp.tanh(cross_gate).reshape(1, KV_HEADS, repeat, 1)
    grad_out = grad_rows.astype(jnp.float32).reshape(tok_rows, KV_HEADS, repeat, HEAD_DIM)
    gate_part = lax.optimization_barrier(jnp.sum(grad_out * cross_mixed, axis=(0, 3))).reshape(HEADS)
    grad_cross = rounded(grad_out * gate_tanh * image_mask)
    cross_query_grad, memory_key_grad, memory_value_grad = attend_back(grad_cross, self_out, memory_keys, memory_values, cross_weights, cross_narrow)
    grad_self = rounded(grad_out + cross_query_grad)
    query_grad, key_grad, value_grad = attend_back(grad_self, query_heads, key_part, value_part, weights, narrow_weights)
    context_part = jnp.concatenate([key_grad.reshape(key_rows, -1), value_grad.reshape(key_rows, -1)], axis=1)
    memory_part = jnp.concatenate([memory_key_grad.reshape(2 * IMG_TOK, -1), memory_value_grad.reshape(2 * IMG_TOK, -1)], axis=1)
    return (query_grad.reshape(tok_rows, -1).astype(jnp.bfloat16), context_part, memory_part, gate_part)

def reference(queries, context, segment_start, memory, image_offset, cross_gate, out_grad):
    doc_count = queries.shape[0]
    tok_rows = TOK_DEV
    flat_count = doc_count * SHARDS
    shard_ids = jnp.arange(SHARDS, dtype=jnp.int32)
    context_blocks = context.reshape(doc_count, SHARDS, tok_rows, -1)
    tail_rows = context_blocks[:, :, tok_rows - WINDOW:]
    earlier = jnp.concatenate([jnp.zeros_like(tail_rows[:, :1]), tail_rows[:, :-1]], axis=1)
    joined_keys = jnp.concatenate([earlier, context_blocks], axis=2).reshape(flat_count, WINDOW + tok_rows, -1)
    is_owner = image_offset < tok_rows
    owner_index = jnp.where(is_owner, shard_ids[None, :], -1).astype(jnp.int32)
    latest = lax.cummax(owner_index, axis=1)
    previous = jnp.concatenate([jnp.full((doc_count, 1), -1, jnp.int32), latest[:, :-1]], axis=1)
    has_prev = previous >= 0
    picked = jax.vmap(lambda images, index: images[index])(memory, jnp.maximum(previous, 0).astype(jnp.int32))
    joined_memory = jnp.concatenate([picked, memory], axis=2).reshape(flat_count, 2 * IMG_TOK, -1)

    def one_shard(item):
        query_rows, key_rows, memory_rows, segment_row, shard_index, offset, owner_flag, prev_flag, grad_rows = item
        allowed = self_mask(shard_index, tok_rows, segment_row)
        cross_allowed, has_image = cross_mask(tok_rows, offset, owner_flag, prev_flag)
        return shard_pass(query_rows, key_rows, memory_rows, allowed, cross_allowed, has_image, cross_gate, grad_rows)
    items = (queries.reshape(flat_count, tok_rows, -1), joined_keys, joined_memory, segment_start.reshape(flat_count, tok_rows), jnp.tile(shard_ids, doc_count), image_offset.reshape(flat_count), is_owner.reshape(flat_count), has_prev.reshape(flat_count), out_grad.reshape(flat_count, tok_rows, -1))
    query_grad, context_part, memory_part, gate_part = lax.map(one_shard, items)
    query_grad = query_grad.reshape(doc_count, SHARDS * tok_rows, -1)
    context_part = context_part.reshape(doc_count, SHARDS, WINDOW + tok_rows, -1)
    returned = jnp.pad(context_part[:, 1:, :WINDOW], ((0, 0), (0, 1), (tok_rows - WINDOW, 0), (0, 0)))
    context_grad = (context_part[:, :, WINDOW:] + returned).astype(jnp.bfloat16).reshape(doc_count, SHARDS * tok_rows, -1)
    memory_part = memory_part.reshape(doc_count, SHARDS, 2 * IMG_TOK, -1)
    carried = memory_part[:, :, :IMG_TOK]
    target = jnp.where(has_prev, previous, SHARDS).astype(jnp.int32)
    flat_target = (jnp.arange(doc_count, dtype=jnp.int32)[:, None] * (SHARDS + 1) + target).reshape(-1).astype(jnp.int32)
    summed = jax.ops.segment_sum(carried.reshape(flat_count, IMG_TOK, -1), flat_target, num_segments=doc_count * (SHARDS + 1))
    summed = summed.reshape(doc_count, SHARDS + 1, IMG_TOK, -1)[:, :SHARDS]
    memory_grad = jnp.where(is_owner[:, :, None, None], memory_part[:, :, IMG_TOK:] + summed, 0.0).astype(jnp.bfloat16)
    gate_tanh = jnp.tanh(cross_gate)
    gate_grad = (1.0 - gate_tanh * gate_tanh) * lax.optimization_barrier(jnp.sum(gate_part, axis=0))
    return (query_grad, context_grad, memory_grad, gate_grad)
```

```python
import functools
import math

import jax
import jax.numpy as jnp
from jax import lax
from jax.experimental import pallas as pl
from jax.experimental.pallas import tpu as pltpu
from jax.sharding import PartitionSpec as P

HEAD_DIM = 128
WINDOW = 64
BLOCK = 4
ROW = 8
SCALE = 1.0 / math.sqrt(HEAD_DIM)
EXP_SCALE = SCALE / math.log(2.0)
MESH = pl.DeviceIdType.MESH
F32 = jnp.float32
BF16 = jnp.bfloat16
HIDDEN = -1e30


def dot_nn(a, b):
    return lax.dot_general(a, b, (((1,), (0,)), ((), ())), preferred_element_type=F32)


def dot_nt(a, b):
    return lax.dot_general(a, b, (((1,), (1,)), ((), ())), preferred_element_type=F32)


def dot_tn(a, b):
    return lax.dot_general(a, b, (((0,), (0,)), ((), ())), preferred_element_type=F32)


def softmax(scores):
    top = jnp.max(scores, axis=-1, keepdims=True)
    powers = jnp.exp2((scores - top) * EXP_SCALE)
    return powers * (1.0 / jnp.sum(powers, axis=-1, keepdims=True))


def stacked(ref, half, group, repeat):
    base = group * (repeat * HEAD_DIM)
    rows = slice(half * WINDOW, (half + 1) * WINDOW)
    return jnp.concatenate(
        [
            ref[rows, pl.ds(pl.multiple_of(base + head * HEAD_DIM, HEAD_DIM), HEAD_DIM)]
            for head in range(repeat)
        ],
        axis=0,
    )


def columns(group, offset=0):
    return pl.ds(pl.multiple_of(offset + group * HEAD_DIM, HEAD_DIM), HEAD_DIM)


def kernel(
    shards,
    docs,
    seg_ref,
    off_ref,
    gate_ref,
    q_hbm,
    c_hbm,
    m_hbm,
    g_hbm,
    qg_hbm,
    cg_hbm,
    mg_hbm,
    gt_ref,
    q_buf,
    g_buf,
    keys,
    images,
    cur_buf,
    prev_buf,
    scat_buf,
    flag_own,
    flag_buf,
    w_ref,
    so_ref,
    gs_ref,
    bias_ref,
    cbias_ref,
    has_ref,
    tanh_ref,
    gacc_ref,
    mt_ref,
    kt_ref,
    qg_buf,
    cg_buf,
    mg_buf,
    to_cur,
    to_prev,
    red_cur,
    red_prev,
    sum_buf,
    halo_out,
    halo_in,
    ga_own,
    ga_in,
    gb_own,
    gb_in,
    gc_own,
    gc_in,
    local_sem,
    send_sem,
    recv_sem,
):
    heads = gate_ref.shape[1]
    tok_rows = q_buf.shape[0]
    width = keys.shape[1]
    key_width = width // 2
    groups = key_width // HEAD_DIM
    repeat = heads // groups
    quarter = m_hbm.shape[0] // BLOCK
    image_rows = m_hbm.shape[0]
    tall = repeat * WINDOW

    me = lax.axis_index("seq")
    doc = lax.axis_index("dp")
    place = lax.rem(me, BLOCK)
    block = me // BLOCK
    blocks = shards // BLOCK
    next_block = lax.rem(block + 1, blocks)
    last_block = lax.rem(block + blocks - 1, blocks)
    y_count = 2 * docs
    z_count = shards // (2 * ROW)
    in_row = lax.rem(me, ROW)
    y_place = doc * 2 + lax.rem(me // ROW, 2)
    z_place = me // (2 * ROW)

    def mate(d):
        return lax.rem(place + d, BLOCK)

    def on_seq(index):
        return {"seq": index, "dp": doc}

    def in_block(which, d):
        return on_seq(which * BLOCK + mate(d))

    def row_peer(d):
        return on_seq(me - in_row + lax.rem(in_row + d, ROW))

    def y_peer(d):
        there = lax.rem(y_place + d, y_count)
        return {
            "seq": z_place * (2 * ROW) + lax.rem(there, 2) * ROW + in_row,
            "dp": there // 2,
        }

    def z_peer(d):
        there = lax.rem(z_place + d, z_count)
        return on_seq(there * (2 * ROW) + lax.rem(me, 2 * ROW))

    sems = [0]

    def remote(src, dst, device):
        at = sems[0]
        sems[0] += 1
        return pltpu.make_async_remote_copy(
            src_ref=src,
            dst_ref=dst,
            send_sem=send_sem.at[at],
            recv_sem=recv_sem.at[at],
            device_id=device,
            device_id_type=MESH,
        )

    barrier = pltpu.get_barrier_semaphore()
    greeted = (
        [in_block(block, d) for d in range(1, BLOCK)]
        + [in_block(next_block, d) for d in range(BLOCK)]
        + [in_block(last_block, d) for d in range(BLOCK)]
        + [y_peer(d) for d in range(1, y_count)]
        + [z_peer(d) for d in range(1, z_count)]
    )
    for device in greeted:
        pl.semaphore_signal(barrier, inc=1, device_id=device, device_id_type=MESH)

    load_keys = pltpu.make_async_copy(
        c_hbm, keys.at[pl.ds(WINDOW, tok_rows)], local_sem.at[0]
    )
    load_q = pltpu.make_async_copy(q_hbm, q_buf, local_sem.at[1])
    load_own = pltpu.make_async_copy(
        m_hbm, images.at[pl.ds(image_rows, image_rows)], local_sem.at[2]
    )
    load_g = pltpu.make_async_copy(g_hbm, g_buf, local_sem.at[3])
    load_keys.start()
    load_q.start()
    load_own.start()
    load_g.start()

    offset = off_ref[0, 0]
    flag_own[...] = jnp.where(jnp.full(flag_own.shape, offset, jnp.int32) < tok_rows, 1.0, 0.0)
    pl.semaphore_wait(barrier, len(greeted))

    flags = [remote(flag_own, flag_buf.at[d - 1], in_block(block, d)) for d in range(1, BLOCK)]
    scatter = [
        remote(
            m_hbm.at[pl.ds(pl.multiple_of(mate(d) * quarter, quarter), quarter)],
            scat_buf.at[d - 1],
            in_block(block, d),
        )
        for d in range(1, BLOCK)
    ]
    halo = remote(
        c_hbm.at[pl.ds(tok_rows - WINDOW, WINDOW)],
        keys.at[pl.ds(0, WINDOW)],
        on_seq(lax.rem(me + 1, shards)),
    )
    for copy in flags + scatter + [halo]:
        copy.start()

    row_id = lax.broadcasted_iota(jnp.int32, (WINDOW, 2 * WINDOW), 0)
    col_id = lax.broadcasted_iota(jnp.int32, (WINDOW, 2 * WINDOW), 1)
    band = (col_id >= row_id) & (col_id <= row_id + WINDOW)
    wide_row = lax.broadcasted_iota(jnp.int32, (tok_rows, tok_rows), 0)
    wide_col = lax.broadcasted_iota(jnp.int32, (tok_rows, tok_rows), 1)
    starts = jnp.sum(
        jnp.where(
            wide_row == wide_col,
            jnp.broadcast_to(seg_ref[...].astype(F32), (tok_rows, tok_rows)),
            0.0,
        ),
        axis=1,
        keepdims=True,
    )
    starts = starts - (me * tok_rows).astype(F32)
    for half in range(2):
        begin = starts[half * WINDOW : (half + 1) * WINDOW]
        key_at = (col_id - (WINDOW if half == 0 else 0)).astype(F32)
        bias_ref[half] = jnp.where(band & (key_at >= begin), 0.0, HIDDEN)
    gate_row = gate_ref[...]
    head_eye = lax.broadcasted_iota(jnp.int32, (heads, heads), 0) == lax.broadcasted_iota(
        jnp.int32, (heads, heads), 1
    )
    gate_col = jnp.sum(
        jnp.where(head_eye, jnp.broadcast_to(gate_row, (heads, heads)), 0.0), axis=1, keepdims=True
    )
    tanh_ref[...] = jnp.tanh(jnp.broadcast_to(gate_col, tanh_ref.shape))

    def self_forward(half, group):
        query = stacked(q_buf, half, group, repeat)
        first = half * WINDOW
        key = keys[first : first + 2 * WINDOW, columns(group)]
        value = keys[first : first + 2 * WINDOW, columns(group, key_width)]
        scores = dot_nt(query, key).reshape(repeat, WINDOW, 2 * WINDOW) + bias_ref[half][None]
        weights = softmax(scores.reshape(tall, 2 * WINDOW))
        w_ref[half, group] = weights
        so_ref[half, group] = dot_nn(weights.astype(BF16), value).astype(BF16)

    load_keys.wait()
    load_q.wait()

    @pl.loop(0, groups)
    def _(group):
        self_forward(1, group)

    for copy in flags + scatter:
        copy.wait_recv()
    load_own.wait()
    own_flag = flag_own[0:1, 0:1]
    picked = own_flag * images[
        pl.ds(pl.multiple_of(image_rows + place * quarter, quarter), quarter), :
    ].astype(F32)
    earlier = jnp.zeros((1, 1), F32)
    for d in range(1, BLOCK):
        flag = flag_buf[d - 1, 0:1, 0:1]
        picked = picked + flag * scat_buf[d - 1].astype(F32)
        earlier = earlier + flag * jnp.where(place >= d, 1.0, 0.0)
    mine = pl.ds(pl.multiple_of(place * quarter, quarter), quarter)
    cur_buf[mine, :] = picked.astype(BF16)
    gather = [
        remote(cur_buf.at[mine], cur_buf.at[mine], in_block(block, d)) for d in range(1, BLOCK)
    ]
    onward = [
        remote(cur_buf.at[mine], prev_buf.at[mine], in_block(next_block, d)) for d in range(BLOCK)
    ]
    for copy in onward + gather:
        copy.start()

    halo.wait_recv()

    @pl.loop(0, groups)
    def _(group):
        self_forward(0, group)

    is_owner = own_flag > 0.5
    has_prev = jnp.maximum(earlier, jnp.where(block > 0, 1.0, 0.0))
    local_row = row_id.astype(F32)
    image_col = col_id < image_rows
    for half in range(2):
        at = local_row + float(half * WINDOW)
        use_own = jnp.where(at >= offset.astype(F32), own_flag, 0.0)
        use_prev = (1.0 - use_own) * has_prev
        cbias_ref[half] = (jnp.where(image_col, use_prev, use_own) - 1.0) * (-HIDDEN)
        has_ref[half] = jnp.maximum(use_own, use_prev)

    for copy in gather + onward:
        copy.wait_recv()
    load_g.wait()
    images[0:image_rows, :] = (
        earlier * cur_buf[...].astype(F32) + (1.0 - earlier) * prev_buf[...].astype(F32)
    ).astype(BF16)

    def cross_half(half, group, key, value):
        self_out = so_ref[half, group]
        grad_out = stacked(g_buf, half, group, repeat)
        scores = dot_nt(self_out, key).reshape(repeat, WINDOW, 2 * image_rows) + cbias_ref[half][None]
        weights = softmax(scores.reshape(tall, 2 * image_rows)).reshape(
            repeat, WINDOW, 2 * image_rows
        )
        narrow = weights.astype(BF16)
        raw = dot_nt(grad_out, value).reshape(repeat, WINDOW, 2 * image_rows)
        has = has_ref[half][None]
        gate_sum = jnp.sum(narrow.astype(F32) * raw * has, axis=1)
        factor = has * tanh_ref[pl.ds(pl.multiple_of(group * repeat, repeat), repeat), :][:, None, :]
        grad_wide = grad_out.astype(F32)
        grad_cross = (grad_wide.reshape(factor.shape) * factor).astype(BF16).reshape(tall, HEAD_DIM)
        grad_weights = raw * factor
        delta = jnp.sum(weights * grad_weights, axis=-1, keepdims=True)
        grad_scores = (
            (weights * (grad_weights - delta)).astype(BF16).reshape(tall, 2 * image_rows)
        )
        query_grad = dot_nn(grad_scores, key) * SCALE
        gs_ref[half, group] = (grad_wide + query_grad).astype(BF16)
        key_term = dot_tn(grad_scores, self_out)
        value_term = dot_tn(narrow.reshape(tall, 2 * image_rows), grad_cross)
        return gate_sum, key_term, value_term

    @pl.loop(0, groups)
    def _(group):
        key = images[:, columns(group)]
        value = images[:, columns(group, key_width)]
        first = cross_half(0, group, key, value)
        second = cross_half(1, group, key, value)
        gacc_ref[pl.ds(pl.multiple_of(group * repeat, repeat), repeat), :] = first[0] + second[0]
        mt_ref[:, columns(group)] = (first[1] + second[1]) * SCALE
        mt_ref[:, columns(group, key_width)] = first[2] + second[2]

    totals = jnp.sum(gacc_ref[...], axis=1, keepdims=True)
    spread = lax.broadcasted_iota(jnp.int32, (heads, 128), 0) == lax.broadcasted_iota(
        jnp.int32, (heads, 128), 1
    )
    gate_line = jnp.sum(jnp.where(spread, totals, 0.0), axis=0, keepdims=True)
    ga_own[...] = jnp.broadcast_to(gate_line, ga_own.shape)
    ga = [remote(ga_own, ga_in.at[d - 1], row_peer(d)) for d in range(1, ROW)]
    for copy in ga:
        copy.start()

    carried = mt_ref[0:image_rows, :]
    to_cur[...] = (carried * earlier).astype(BF16)
    to_prev[...] = (carried * (1.0 - earlier)).astype(BF16)

    def part(d):
        return pl.ds(pl.multiple_of(mate(d) * quarter, quarter), quarter)

    reduce_prev = [
        remote(to_prev.at[part(d)], red_prev.at[d], in_block(last_block, d)) for d in range(BLOCK)
    ]
    reduce_cur = [
        remote(to_cur.at[part(d)], red_cur.at[d - 1], in_block(block, d)) for d in range(1, BLOCK)
    ]
    for copy in reduce_prev + reduce_cur:
        copy.start()

    def self_backward(half, group):
        query = stacked(q_buf, half, group, repeat)
        first = half * WINDOW
        key = keys[first : first + 2 * WINDOW, columns(group)]
        value = keys[first : first + 2 * WINDOW, columns(group, key_width)]
        weights = w_ref[half, group]
        grad_self = gs_ref[half, group]
        grad_weights = dot_nt(grad_self, value)
        delta = jnp.sum(weights * grad_weights, axis=-1, keepdims=True)
        grad_scores = (weights * (grad_weights - delta)).astype(BF16)
        query_grad = (dot_nn(grad_scores, key) * SCALE).astype(BF16)
        base = group * (repeat * HEAD_DIM)
        for head in range(repeat):
            qg_buf[
                first : first + WINDOW,
                pl.ds(pl.multiple_of(base + head * HEAD_DIM, HEAD_DIM), HEAD_DIM),
            ] = query_grad[head * WINDOW : (head + 1) * WINDOW]
        kt_ref[half, :, columns(group)] = dot_tn(grad_scores, query) * SCALE
        kt_ref[half, :, columns(group, key_width)] = dot_tn(weights.astype(BF16), grad_self)

    @pl.loop(0, groups)
    def _(group):
        self_backward(0, group)

    halo_out[...] = kt_ref[0, 0:WINDOW, :].astype(BF16)
    halo_back = remote(halo_out, halo_in, on_seq(lax.rem(me + shards - 1, shards)))
    halo_back.start()
    out_low = pltpu.make_async_copy(
        qg_buf.at[pl.ds(0, WINDOW)], qg_hbm.at[pl.ds(0, WINDOW)], local_sem.at[4]
    )
    out_low.start()

    for copy in ga:
        copy.wait_recv()
    gate_line = ga_own[...]
    for d in range(1, ROW):
        gate_line = gate_line + ga_in[d - 1]
    gb_own[...] = gate_line
    gb = [remote(gb_own, gb_in.at[d - 1], y_peer(d)) for d in range(1, y_count)]
    for copy in gb:
        copy.start()

    for copy in reduce_cur + reduce_prev:
        copy.wait_recv()
    summed = to_cur[mine, :].astype(F32) + red_prev[0].astype(F32)
    for d in range(1, BLOCK):
        summed = summed + red_cur[d - 1].astype(F32) + red_prev[d].astype(F32)
    sum_buf[mine, :] = summed.astype(BF16)
    give = [
        remote(sum_buf.at[mine], sum_buf.at[mine], in_block(block, d)) for d in range(1, BLOCK)
    ]
    for copy in give:
        copy.start()

    @pl.loop(0, groups)
    def _(group):
        self_backward(1, group)

    out_high = pltpu.make_async_copy(
        qg_buf.at[pl.ds(WINDOW, WINDOW)], qg_hbm.at[pl.ds(WINDOW, WINDOW)], local_sem.at[5]
    )
    out_high.start()

    for copy in gb:
        copy.wait_recv()
    gate_line = gb_own[...]
    for d in range(1, y_count):
        gate_line = gate_line + gb_in[d - 1]
    gc_own[...] = gate_line
    gc = [remote(gc_own, gc_in.at[d - 1], z_peer(d)) for d in range(1, z_count)]
    for copy in gc:
        copy.start()

    halo_back.wait_recv()
    cg_buf[0:WINDOW, :] = (kt_ref[0, WINDOW : 2 * WINDOW, :] + kt_ref[1, 0:WINDOW, :]).astype(BF16)
    cg_buf[WINDOW : 2 * WINDOW, :] = (
        kt_ref[1, WINDOW : 2 * WINDOW, :] + halo_in[...].astype(F32)
    ).astype(BF16)
    out_context = pltpu.make_async_copy(cg_buf, cg_hbm, local_sem.at[6])
    out_context.start()

    for copy in give:
        copy.wait_recv()
    mg_buf[...] = (
        (mt_ref[image_rows : 2 * image_rows, :] + sum_buf[...].astype(F32)) * own_flag
    ).astype(BF16)
    out_memory = pltpu.make_async_copy(mg_buf, mg_hbm, local_sem.at[7])
    out_memory.start()

    for copy in gc:
        copy.wait_recv()
    gate_line = gc_own[...]
    for d in range(1, z_count):
        gate_line = gate_line + gc_in[d - 1]
    gate_tanh = jnp.tanh(gate_row)
    gt_ref[...] = (1.0 - gate_tanh * gate_tanh) * gate_line[0:1, 0:heads]

    for copy in (
        flags + scatter + [halo] + gather + onward + ga + reduce_prev + reduce_cur
        + [halo_back] + gb + give + gc
    ):
        copy.wait_send()
    out_low.wait()
    out_high.wait()
    out_context.wait()
    out_memory.wait()


def on_device(shards, docs, queries, context, segment_start, memory, image_offset, cross_gate, out_grad):
    tok_rows, model = queries.shape[1:]
    width = context.shape[2]
    image_rows = memory.shape[2]
    heads = cross_gate.shape[0]
    groups = width // 2 // HEAD_DIM
    repeat = heads // groups
    quarter = image_rows // BLOCK
    tall = repeat * WINDOW
    y_count = 2 * docs
    z_count = shards // (2 * ROW)
    copies = 3 + 3 + 1 + 3 + 4 + (ROW - 1) + 4 + 3 + 1 + (y_count - 1) + 3 + (z_count - 1)
    anywhere = pl.BlockSpec(memory_space=pl.ANY)
    vmem = pl.BlockSpec(memory_space=pltpu.VMEM)
    smem = pl.BlockSpec(memory_space=pltpu.SMEM)

    def buf(*shape):
        return pltpu.VMEM(shape, BF16)

    def wide(*shape):
        return pltpu.VMEM(shape, F32)

    query_grad, context_grad, memory_grad, gate_grad = pl.pallas_call(
        functools.partial(kernel, shards, docs),
        out_shape=(
            jax.ShapeDtypeStruct((tok_rows, model), BF16),
            jax.ShapeDtypeStruct((tok_rows, width), BF16),
            jax.ShapeDtypeStruct((image_rows, width), BF16),
            jax.ShapeDtypeStruct((1, heads), F32),
        ),
        in_specs=[vmem, smem, vmem, anywhere, anywhere, anywhere, anywhere],
        out_specs=(anywhere, anywhere, anywhere, vmem),
        scratch_shapes=[
            buf(tok_rows, model),
            buf(tok_rows, model),
            buf(WINDOW + tok_rows, width),
            buf(2 * image_rows, width),
            buf(image_rows, width),
            buf(image_rows, width),
            buf(BLOCK - 1, quarter, width),
            wide(8, 128),
            wide(BLOCK - 1, 8, 128),
            wide(2, groups, tall, 2 * WINDOW),
            buf(2, groups, tall, HEAD_DIM),
            buf(2, groups, tall, HEAD_DIM),
            wide(2, WINDOW, 2 * WINDOW),
            wide(2, WINDOW, 2 * image_rows),
            wide(2, WINDOW, 2 * image_rows),
            wide(heads, 128),
            wide(heads, 128),
            wide(2 * image_rows, width),
            wide(2, 2 * WINDOW, width),
            buf(tok_rows, model),
            buf(tok_rows, width),
            buf(image_rows, width),
            buf(image_rows, width),
            buf(image_rows, width),
            buf(BLOCK - 1, quarter, width),
            buf(BLOCK, quarter, width),
            buf(image_rows, width),
            buf(WINDOW, width),
            buf(WINDOW, width),
            wide(8, 128),
            wide(ROW - 1, 8, 128),
            wide(8, 128),
            wide(max(y_count - 1, 1), 8, 128),
            wide(8, 128),
            wide(max(z_count - 1, 1), 8, 128),
            pltpu.SemaphoreType.DMA((8,)),
            pltpu.SemaphoreType.DMA((copies,)),
            pltpu.SemaphoreType.DMA((copies,)),
        ],
        compiler_params=pltpu.CompilerParams(
            collective_id=0, has_side_effects=True, vmem_limit_bytes=60000 * 1024
        ),
    )(
        segment_start,
        image_offset,
        cross_gate.reshape(1, heads),
        queries[0],
        context[0],
        memory[0, 0],
        out_grad[0],
    )
    return query_grad[None], context_grad[None], memory_grad[None, None], gate_grad.reshape(heads)


def solution(mesh):
    placed = (
        P("dp", "seq", None),
        P("dp", "seq", None),
        P("dp", "seq"),
        P("dp", "seq", None, None),
        P("dp", "seq"),
        P(),
        P("dp", "seq", None),
    )
    return jax.shard_map(
        functools.partial(on_device, mesh.shape["seq"], mesh.shape["dp"]),
        mesh=mesh,
        in_specs=placed,
        out_specs=(P("dp", "seq", None), P("dp", "seq", None), P("dp", "seq", None, None), P()),
        check_vma=False,
    )
```

```python
import functools
import math

import jax
import jax.numpy as jnp
from jax import lax
from jax.experimental import pallas as pl
from jax.experimental.pallas import tpu as pltpu
from jax.sharding import PartitionSpec as P

HEAD_DIM = 128
WINDOW = 64
BLOCK = 4
ROW = 8
SCALE = 1.0 / math.sqrt(HEAD_DIM)
EXP_SCALE = SCALE / math.log(2.0)
MESH = pl.DeviceIdType.MESH
F32 = jnp.float32
BF16 = jnp.bfloat16
HIDDEN = -1e30


def dot_nn(a, b):
    return lax.dot_general(a, b, (((1,), (0,)), ((), ())), preferred_element_type=F32)


def dot_nt(a, b):
    return lax.dot_general(a, b, (((1,), (1,)), ((), ())), preferred_element_type=F32)


def dot_tn(a, b):
    return lax.dot_general(a, b, (((0,), (0,)), ((), ())), preferred_element_type=F32)


def softmax(scores):
    top = jnp.max(scores, axis=-1, keepdims=True)
    powers = jnp.exp2((scores - top) * EXP_SCALE)
    return powers * (1.0 / jnp.sum(powers, axis=-1, keepdims=True))


def stacked(ref, half, group, repeat):
    base = group * (repeat * HEAD_DIM)
    rows = slice(half * WINDOW, (half + 1) * WINDOW)
    return jnp.concatenate(
        [
            ref[rows, pl.ds(pl.multiple_of(base + head * HEAD_DIM, HEAD_DIM), HEAD_DIM)]
            for head in range(repeat)
        ],
        axis=0,
    )


def columns(group, offset=0):
    return pl.ds(pl.multiple_of(offset + group * HEAD_DIM, HEAD_DIM), HEAD_DIM)


def kernel(
    shards,
    docs,
    seg_ref,
    off_ref,
    gate_ref,
    q_hbm,
    c_hbm,
    m_hbm,
    g_hbm,
    qg_buf,
    cg_buf,
    mg_buf,
    gt_ref,
    q_buf,
    g_buf,
    keys,
    images,
    cur_buf,
    prev_buf,
    scat_buf,
    flag_own,
    flag_buf,
    w_ref,
    so_ref,
    gs_ref,
    bias_ref,
    cbias_ref,
    has_ref,
    xw_ref,
    raw_ref,
    tanh_ref,
    gacc_ref,
    mt_ref,
    kt_ref,
    to_cur,
    to_prev,
    red_cur,
    red_prev,
    sum_buf,
    halo_out,
    halo_in,
    ga_own,
    ga_in,
    gb_own,
    gb_in,
    gc_own,
    gc_in,
    local_sem,
    send_sem,
    recv_sem,
):
    heads = gate_ref.shape[1]
    tok_rows = q_buf.shape[0]
    width = keys.shape[1]
    key_width = width // 2
    groups = key_width // HEAD_DIM
    repeat = heads // groups
    quarter = m_hbm.shape[0] // BLOCK
    image_rows = m_hbm.shape[0]
    tall = repeat * WINDOW

    me = lax.axis_index("seq")
    doc = lax.axis_index("dp")
    place = lax.rem(me, BLOCK)
    block = me // BLOCK
    blocks = shards // BLOCK
    next_block = lax.rem(block + 1, blocks)
    last_block = lax.rem(block + blocks - 1, blocks)
    y_count = 2 * docs
    z_count = shards // (2 * ROW)
    in_row = lax.rem(me, ROW)
    y_place = doc * 2 + lax.rem(me // ROW, 2)
    z_place = me // (2 * ROW)

    def mate(d):
        return lax.rem(place + d, BLOCK)

    def on_seq(index):
        return {"seq": index, "dp": doc}

    def in_block(which, d):
        return on_seq(which * BLOCK + mate(d))

    def row_peer(d):
        return on_seq(me - in_row + lax.rem(in_row + d, ROW))

    def y_peer(d):
        there = lax.rem(y_place + d, y_count)
        return {
            "seq": z_place * (2 * ROW) + lax.rem(there, 2) * ROW + in_row,
            "dp": there // 2,
        }

    def z_peer(d):
        there = lax.rem(z_place + d, z_count)
        return on_seq(there * (2 * ROW) + lax.rem(me, 2 * ROW))

    sems = [0]

    def remote(src, dst, device):
        at = sems[0]
        sems[0] += 1
        return pltpu.make_async_remote_copy(
            src_ref=src,
            dst_ref=dst,
            send_sem=send_sem.at[at],
            recv_sem=recv_sem.at[at],
            device_id=device,
            device_id_type=MESH,
        )

    barrier = pltpu.get_barrier_semaphore()
    greeted = (
        [in_block(block, d) for d in range(1, BLOCK)]
        + [in_block(next_block, d) for d in range(BLOCK)]
        + [in_block(last_block, d) for d in range(BLOCK)]
        + [y_peer(d) for d in range(1, y_count)]
        + [z_peer(d) for d in range(1, z_count)]
    )
    for device in greeted:
        pl.semaphore_signal(barrier, inc=1, device_id=device, device_id_type=MESH)

    load_keys = pltpu.make_async_copy(
        c_hbm, keys.at[pl.ds(WINDOW, tok_rows)], local_sem.at[0]
    )
    load_q = pltpu.make_async_copy(q_hbm, q_buf, local_sem.at[1])
    load_own = pltpu.make_async_copy(
        m_hbm, images.at[pl.ds(image_rows, image_rows)], local_sem.at[2]
    )
    load_g = pltpu.make_async_copy(g_hbm, g_buf, local_sem.at[3])
    load_keys.start()
    load_q.start()
    load_own.start()
    load_g.start()

    offset = off_ref[...]
    flag_own[...] = jnp.where(jnp.broadcast_to(offset, flag_own.shape) < tok_rows, 1.0, 0.0)
    pl.semaphore_wait(barrier, len(greeted))

    flags = [remote(flag_own, flag_buf.at[d - 1], in_block(block, d)) for d in range(1, BLOCK)]
    scatter = [
        remote(
            m_hbm.at[pl.ds(pl.multiple_of(mate(d) * quarter, quarter), quarter)],
            scat_buf.at[d - 1],
            in_block(block, d),
        )
        for d in range(1, BLOCK)
    ]
    halo = remote(
        c_hbm.at[pl.ds(tok_rows - WINDOW, WINDOW)],
        keys.at[pl.ds(0, WINDOW)],
        on_seq(lax.rem(me + 1, shards)),
    )
    for copy in flags + scatter + [halo]:
        copy.start()

    row_id = lax.broadcasted_iota(jnp.int32, (WINDOW, 2 * WINDOW), 0)
    col_id = lax.broadcasted_iota(jnp.int32, (WINDOW, 2 * WINDOW), 1)
    band = (col_id >= row_id) & (col_id <= row_id + WINDOW)
    wide_row = lax.broadcasted_iota(jnp.int32, (tok_rows, tok_rows), 0)
    wide_col = lax.broadcasted_iota(jnp.int32, (tok_rows, tok_rows), 1)
    starts = jnp.sum(
        jnp.where(
            wide_row == wide_col,
            jnp.broadcast_to(seg_ref[...].astype(F32), (tok_rows, tok_rows)),
            0.0,
        ),
        axis=1,
        keepdims=True,
    )
    starts = starts - (me * tok_rows).astype(F32)
    for half in range(2):
        begin = starts[half * WINDOW : (half + 1) * WINDOW]
        key_at = (col_id - (WINDOW if half == 0 else 0)).astype(F32)
        bias_ref[half] = jnp.where(band & (key_at >= begin), 0.0, HIDDEN)
    gate_row = gate_ref[...]
    head_eye = lax.broadcasted_iota(jnp.int32, (heads, heads), 0) == lax.broadcasted_iota(
        jnp.int32, (heads, heads), 1
    )
    gate_col = jnp.sum(
        jnp.where(head_eye, jnp.broadcast_to(gate_row, (heads, heads)), 0.0), axis=1, keepdims=True
    )
    tanh_ref[...] = jnp.tanh(jnp.broadcast_to(gate_col, tanh_ref.shape))

    def self_forward(half, group):
        query = stacked(q_buf, half, group, repeat)
        first = half * WINDOW
        key = keys[first : first + 2 * WINDOW, columns(group)]
        value = keys[first : first + 2 * WINDOW, columns(group, key_width)]
        scores = dot_nt(query, key).reshape(repeat, WINDOW, 2 * WINDOW) + bias_ref[half][None]
        weights = softmax(scores.reshape(tall, 2 * WINDOW))
        w_ref[half, group] = weights
        so_ref[half, group] = dot_nn(weights.astype(BF16), value).astype(BF16)

    load_keys.wait()
    load_q.wait()

    @pl.loop(0, groups)
    def _(group):
        self_forward(1, group)

    for copy in flags + scatter:
        copy.wait_recv()
    load_own.wait()
    own_flag = flag_own[0:1, 0:1]
    picked = own_flag * images[
        pl.ds(pl.multiple_of(image_rows + place * quarter, quarter), quarter), :
    ].astype(F32)
    earlier = jnp.zeros((1, 1), F32)
    for d in range(1, BLOCK):
        flag = flag_buf[d - 1, 0:1, 0:1]
        picked = picked + flag * scat_buf[d - 1].astype(F32)
        earlier = earlier + flag * jnp.where(place >= d, 1.0, 0.0)
    mine = pl.ds(pl.multiple_of(place * quarter, quarter), quarter)
    cur_buf[mine, :] = picked.astype(BF16)
    gather = [
        remote(cur_buf.at[mine], cur_buf.at[mine], in_block(block, d)) for d in range(1, BLOCK)
    ]
    onward = [
        remote(cur_buf.at[mine], prev_buf.at[mine], in_block(next_block, d)) for d in range(BLOCK)
    ]
    for copy in onward + gather:
        copy.start()

    has_prev = jnp.maximum(earlier, jnp.where(block > 0, 1.0, 0.0))
    local_row = row_id.astype(F32)
    image_col = col_id < image_rows
    for half in range(2):
        at = local_row + float(half * WINDOW)
        use_own = jnp.where(at >= offset.astype(F32), own_flag, 0.0)
        use_prev = (1.0 - use_own) * has_prev
        cbias_ref[half] = (jnp.where(image_col, use_prev, use_own) - 1.0) * (-HIDDEN)
        has_ref[half] = jnp.maximum(use_own, use_prev)

    halo.wait_recv()

    @pl.loop(0, groups)
    def _(group):
        self_forward(0, group)

    for copy in gather + onward:
        copy.wait_recv()
    load_g.wait()
    images[0:image_rows, :] = (
        earlier * cur_buf[...].astype(F32) + (1.0 - earlier) * prev_buf[...].astype(F32)
    ).astype(BF16)

    def cross_forward(half, group, key, value):
        self_out = so_ref[half, group]
        grad_out = stacked(g_buf, half, group, repeat)
        scores = dot_nt(self_out, key).reshape(repeat, WINDOW, 2 * image_rows)
        weights = softmax((scores + cbias_ref[half][None]).reshape(tall, 2 * image_rows))
        raw = dot_nt(grad_out, value)
        xw_ref[half, group] = weights
        raw_ref[half, group] = raw
        terms = (weights.astype(BF16).astype(F32) * raw).reshape(repeat, WINDOW, 2 * image_rows)
        return jnp.sum(terms * has_ref[half][None], axis=1)

    @pl.loop(0, groups)
    def _(group):
        key = images[:, columns(group)]
        value = images[:, columns(group, key_width)]
        own_heads = pl.ds(pl.multiple_of(group * repeat, repeat), repeat)
        gacc_ref[own_heads, :] = cross_forward(0, group, key, value) + cross_forward(
            1, group, key, value
        )

    totals = jnp.sum(gacc_ref[...], axis=1, keepdims=True)
    spread = lax.broadcasted_iota(jnp.int32, (heads, 128), 0) == lax.broadcasted_iota(
        jnp.int32, (heads, 128), 1
    )
    gate_line = jnp.sum(jnp.where(spread, totals, 0.0), axis=0, keepdims=True)
    ga_own[...] = jnp.broadcast_to(gate_line, ga_own.shape)
    ga = [remote(ga_own, ga_in.at[d - 1], row_peer(d)) for d in range(1, ROW)]
    for copy in ga:
        copy.start()

    def cross_backward(half, group, key):
        self_out = so_ref[half, group]
        grad_out = stacked(g_buf, half, group, repeat).astype(F32)
        weights = xw_ref[half, group]
        own_heads = pl.ds(pl.multiple_of(group * repeat, repeat), repeat)
        factor = has_ref[half][None] * tanh_ref[own_heads, :][:, None, :]
        factor = factor.reshape(tall, 2 * image_rows)
        grad_cross = (grad_out * factor).astype(BF16)
        grad_weights = raw_ref[half, group] * factor
        delta = jnp.sum(weights * grad_weights, axis=-1, keepdims=True)
        grad_scores = (weights * (grad_weights - delta)).astype(BF16)
        gs_ref[half, group] = (grad_out + dot_nn(grad_scores, key) * SCALE).astype(BF16)
        return dot_tn(grad_scores, self_out), dot_tn(weights.astype(BF16), grad_cross)

    @pl.loop(0, groups)
    def _(group):
        key = images[:, columns(group)]
        first = cross_backward(0, group, key)
        second = cross_backward(1, group, key)
        mt_ref[:, columns(group)] = (first[0] + second[0]) * SCALE
        mt_ref[:, columns(group, key_width)] = first[1] + second[1]

    carried = mt_ref[0:image_rows, :]
    to_cur[...] = (carried * earlier).astype(BF16)
    to_prev[...] = (carried * (1.0 - earlier)).astype(BF16)

    def part(d):
        return pl.ds(pl.multiple_of(mate(d) * quarter, quarter), quarter)

    reduce_prev = [
        remote(to_prev.at[part(d)], red_prev.at[d], in_block(last_block, d)) for d in range(BLOCK)
    ]
    reduce_cur = [
        remote(to_cur.at[part(d)], red_cur.at[d - 1], in_block(block, d)) for d in range(1, BLOCK)
    ]
    for copy in reduce_prev + reduce_cur:
        copy.start()

    for copy in ga:
        copy.wait_recv()
    gate_line = ga_own[...]
    for d in range(1, ROW):
        gate_line = gate_line + ga_in[d - 1]
    gb_own[...] = gate_line
    gb = [remote(gb_own, gb_in.at[d - 1], y_peer(d)) for d in range(1, y_count)]
    for copy in gb:
        copy.start()

    def self_backward(half, group):
        query = stacked(q_buf, half, group, repeat)
        first = half * WINDOW
        key = keys[first : first + 2 * WINDOW, columns(group)]
        value = keys[first : first + 2 * WINDOW, columns(group, key_width)]
        weights = w_ref[half, group]
        grad_self = gs_ref[half, group]
        grad_weights = dot_nt(grad_self, value)
        delta = jnp.sum(weights * grad_weights, axis=-1, keepdims=True)
        grad_scores = (weights * (grad_weights - delta)).astype(BF16)
        query_grad = (dot_nn(grad_scores, key) * SCALE).astype(BF16)
        base = group * (repeat * HEAD_DIM)
        for head in range(repeat):
            qg_buf[
                first : first + WINDOW,
                pl.ds(pl.multiple_of(base + head * HEAD_DIM, HEAD_DIM), HEAD_DIM),
            ] = query_grad[head * WINDOW : (head + 1) * WINDOW]
        kt_ref[half, :, columns(group)] = dot_tn(grad_scores, query) * SCALE
        kt_ref[half, :, columns(group, key_width)] = dot_tn(weights.astype(BF16), grad_self)

    @pl.loop(0, groups)
    def _(group):
        self_backward(0, group)
        self_backward(1, group)

    halo_out[...] = kt_ref[0, 0:WINDOW, :].astype(BF16)
    halo_back = remote(halo_out, halo_in, on_seq(lax.rem(me + shards - 1, shards)))
    halo_back.start()

    for copy in gb:
        copy.wait_recv()
    gate_line = gb_own[...]
    for d in range(1, y_count):
        gate_line = gate_line + gb_in[d - 1]
    gc_own[...] = gate_line
    gc = [remote(gc_own, gc_in.at[d - 1], z_peer(d)) for d in range(1, z_count)]
    for copy in gc:
        copy.start()

    for copy in reduce_cur + reduce_prev:
        copy.wait_recv()
    summed = to_cur[mine, :].astype(F32) + red_prev[0].astype(F32)
    for d in range(1, BLOCK):
        summed = summed + red_cur[d - 1].astype(F32) + red_prev[d].astype(F32)
    sum_buf[mine, :] = summed.astype(BF16)
    give = [
        remote(sum_buf.at[mine], sum_buf.at[mine], in_block(block, d)) for d in range(1, BLOCK)
    ]
    for copy in give:
        copy.start()

    halo_back.wait_recv()
    cg_buf[0:WINDOW, :] = (kt_ref[0, WINDOW : 2 * WINDOW, :] + kt_ref[1, 0:WINDOW, :]).astype(BF16)
    cg_buf[WINDOW : 2 * WINDOW, :] = (
        kt_ref[1, WINDOW : 2 * WINDOW, :] + halo_in[...].astype(F32)
    ).astype(BF16)

    for copy in give:
        copy.wait_recv()
    mg_buf[...] = (
        (mt_ref[image_rows : 2 * image_rows, :] + sum_buf[...].astype(F32)) * own_flag
    ).astype(BF16)

    for copy in gc:
        copy.wait_recv()
    gate_line = gc_own[...]
    for d in range(1, z_count):
        gate_line = gate_line + gc_in[d - 1]
    gate_tanh = jnp.tanh(gate_row)
    gt_ref[...] = (1.0 - gate_tanh * gate_tanh) * gate_line[0:1, 0:heads]

    for copy in (
        flags + scatter + [halo] + gather + onward + ga + reduce_prev + reduce_cur
        + [halo_back] + gb + give + gc
    ):
        copy.wait_send()


def on_device(shards, docs, queries, context, segment_start, memory, image_offset, cross_gate, out_grad):
    tok_rows, model = queries.shape[1:]
    width = context.shape[2]
    image_rows = memory.shape[2]
    heads = cross_gate.shape[0]
    groups = width // 2 // HEAD_DIM
    repeat = heads // groups
    quarter = image_rows // BLOCK
    tall = repeat * WINDOW
    y_count = 2 * docs
    z_count = shards // (2 * ROW)
    copies = 3 + 3 + 1 + 3 + 4 + (ROW - 1) + 4 + 3 + 1 + (y_count - 1) + 3 + (z_count - 1)
    anywhere = pl.BlockSpec(memory_space=pl.ANY)
    vmem = pl.BlockSpec(memory_space=pltpu.VMEM)

    def buf(*shape):
        return pltpu.VMEM(shape, BF16)

    def wide(*shape):
        return pltpu.VMEM(shape, F32)

    query_grad, context_grad, memory_grad, gate_grad = pl.pallas_call(
        functools.partial(kernel, shards, docs),
        out_shape=(
            pltpu.VMEM((tok_rows, model), BF16),
            pltpu.VMEM((tok_rows, width), BF16),
            pltpu.VMEM((image_rows, width), BF16),
            pltpu.VMEM((1, heads), F32),
        ),
        in_specs=[vmem, vmem, vmem, anywhere, anywhere, anywhere, anywhere],
        out_specs=(vmem, vmem, vmem, vmem),
        scratch_shapes=[
            buf(tok_rows, model),
            buf(tok_rows, model),
            buf(WINDOW + tok_rows, width),
            buf(2 * image_rows, width),
            buf(image_rows, width),
            buf(image_rows, width),
            buf(BLOCK - 1, quarter, width),
            wide(8, 128),
            wide(BLOCK - 1, 8, 128),
            wide(2, groups, tall, 2 * WINDOW),
            buf(2, groups, tall, HEAD_DIM),
            buf(2, groups, tall, HEAD_DIM),
            wide(2, WINDOW, 2 * WINDOW),
            wide(2, WINDOW, 2 * image_rows),
            wide(2, WINDOW, 2 * image_rows),
            wide(2, groups, tall, 2 * image_rows),
            wide(2, groups, tall, 2 * image_rows),
            wide(heads, 128),
            wide(heads, 128),
            wide(2 * image_rows, width),
            wide(2, 2 * WINDOW, width),
            buf(image_rows, width),
            buf(image_rows, width),
            buf(BLOCK - 1, quarter, width),
            buf(BLOCK, quarter, width),
            buf(image_rows, width),
            buf(WINDOW, width),
            buf(WINDOW, width),
            wide(8, 128),
            wide(ROW - 1, 8, 128),
            wide(8, 128),
            wide(max(y_count - 1, 1), 8, 128),
            wide(8, 128),
            wide(max(z_count - 1, 1), 8, 128),
            pltpu.SemaphoreType.DMA((4,)),
            pltpu.SemaphoreType.DMA((copies,)),
            pltpu.SemaphoreType.DMA((copies,)),
        ],
        compiler_params=pltpu.CompilerParams(
            collective_id=0, has_side_effects=True, vmem_limit_bytes=60000 * 1024
        ),
    )(
        segment_start,
        image_offset,
        cross_gate.reshape(1, heads),
        queries[0],
        context[0],
        memory[0, 0],
        out_grad[0],
    )
    return query_grad[None], context_grad[None], memory_grad[None, None], gate_grad.reshape(heads)


def solution(mesh):
    placed = (
        P("dp", "seq", None),
        P("dp", "seq", None),
        P("dp", "seq"),
        P("dp", "seq", None, None),
        P("dp", "seq"),
        P(),
        P("dp", "seq", None),
    )
    return jax.shard_map(
        functools.partial(on_device, mesh.shape["seq"], mesh.shape["dp"]),
        mesh=mesh,
        in_specs=placed,
        out_specs=(P("dp", "seq", None), P("dp", "seq", None), P("dp", "seq", None, None), P()),
        check_vma=False,
    )
```
